32 devices in a mesh: grp: 2 (over x), tok: 16 (over z, y, core).
Axes of the slice: x: 2, y: 2, z: 4, core: 2. Of those that a mesh axis runs over, the one named last changes fastest.
Arguments:
- frames: bfloat16 [256, 48, 4096], P(('grp', 'tok')), parts along dimension 0, may hold values from -6 to 6
- clip_lengths: int32 [8], P('grp'), parts along dimension 0, may hold values from 1 to 56, as said below
- sequence_slot_map: int32 [2048], P(('grp', 'tok')), parts along dimension 0, may hold values from 0 to 1023, as said below
- stem_weight: bfloat16 [128, 48], replicated, may hold values from -0.875 to 0.875
- time_weight: bfloat16 [3, 128, 128], replicated, may hold values from -0.3125 to 0.3125
- norm_gain: float32 [128], replicated, may hold values from 0.1 to 1.9
- mid_weight: bfloat16 [512, 2048], replicated, may hold values from -0.125 to 0.125
- latent_weight: bfloat16 [16, 4096], replicated, may hold values from -0.09375 to 0.09375
- patch_embed_weight: bfloat16 [64, 2048], replicated, may hold values from -0.75 to 0.75
Outputs:
- dit_rows: bfloat16 [2048, 2048], P(('grp', 'tok')), parts along dimension 0
The draws below stay inside these ranges and needn't reach their ends.
There are 2 independent parts, one for each index of `grp`. The reference program is written for one: setup_inputs(seed, part) draws one part's arguments, and reference() takes and returns one part's arrays. A program takes and returns all parts, laid end to end along the dimension named above; an argument that names none is the same for every part. Nothing has to cross between parts.
Inputs may be any that keep to these rules, and one draw needn't show every extreme that they name: `clip_lengths`: clips fill the 16 slabs in order: the counts ceil(length / 8) sum to 16. `sequence_slot_map`: A permutation of the 1024 sequence slots. The rows of one slab send at most 8 rows to the slots of any one slab (exactly 8 to some), and how many slab s sends to slab (s + k) mod 16 depends on k only.
All inputs are finite; a program needn't handle non-finite values.
Results may differ from the reference program's by a relative error of at most 0.0071.
Values may be sent and summed in bfloat16 or wider, within the bound.
No kernel may reach another device: no remote copies, remote signals or barrier semaphores. Data moves between devices by JAX's collectives and lax.ppermute only.
A program may use at most 128 MiB of HBM per device.

```python
import jax
import jax.numpy as jnp
from jax import lax

CIN = 48
C1 = 128
C2 = 512
LATC = 16
DIFFUSION_WIDTH = 2048
FRAMES = 8
LS = 16
POS = 4096
PATCH_FEATURES = 64
SLAB_ROW_COUNT = 64
CAP = 8
CLIPS = 4
TFRAMES = 128
N_TOK = 16


def draw_clip_lengths(key, part):
    keys = jax.random.split(jax.random.fold_in(key, 11), 3)
    order = jax.random.permutation(keys[0], CLIPS).astype(jnp.int32)
    pairs = CLIPS // 2
    moved = jax.random.randint(keys[1], (pairs,), 0, 4).astype(jnp.int32)
    moved = moved.at[0].set(3)
    counts = jnp.full((CLIPS,), 4, jnp.int32)
    counts = counts.at[order[0:2 * pairs:2]].add(moved)
    counts = counts.at[order[1:2 * pairs:2]].add(-moved)
    tails = jax.random.randint(keys[2], (CLIPS,), 1, 9).astype(jnp.int32)
    tails = tails.at[order[0]].set(8)
    tails = tails.at[order[1]].set(1)
    return (8 * (counts - 1) + tails).astype(jnp.int32)


def draw_sequence_slot_map(key, part):
    keys = jax.random.split(jax.random.fold_in(key, 23), 4)
    rest = jax.random.permutation(keys[0], N_TOK * CAP - CAP) + CAP
    chosen = jnp.concatenate([jnp.arange(CAP, dtype=jnp.int32), rest[:SLAB_ROW_COUNT - CAP].astype(jnp.int32)])
    groups = jnp.sort(chosen) // CAP
    offsets = jax.random.permutation(keys[1], N_TOK).astype(jnp.int32)
    slab_ids = jnp.arange(N_TOK, dtype=jnp.int32)
    arrival = jax.vmap(lambda s: jax.random.permutation(jax.random.fold_in(keys[3], s), SLAB_ROW_COUNT))(slab_ids).astype(jnp.int32)
    slot_position = jnp.arange(SLAB_ROW_COUNT, dtype=jnp.int32)

    def one_source(source):
        order = jax.random.permutation(jax.random.fold_in(keys[2], source), SLAB_ROW_COUNT)
        target = (source + offsets[groups]) % N_TOK
        slots = target * SLAB_ROW_COUNT + arrival[target, slot_position]
        return jnp.zeros((SLAB_ROW_COUNT,), jnp.int32).at[order].set(slots.astype(jnp.int32))
    return jax.vmap(one_source)(slab_ids).reshape(N_TOK * SLAB_ROW_COUNT)


def block_scale(stream_key, shape, cuts, smallest, top_value):
    def one(position, blocks):
        steps = jax.random.uniform(jax.random.fold_in(jax.random.fold_in(stream_key, 6), position), (blocks,), jnp.float32, smallest / len(cuts), top_value / len(cuts))
        return jnp.repeat(jnp.exp(steps), shape[position] // blocks).reshape((-1,) + (1,) * (len(shape) - position - 1))

    level = one(*cuts[0])
    for cut in cuts[1:]:
        level = level * one(*cut)
    return level


def gaussian(key, dims, scale, reach, shards=(), kind=jnp.bfloat16):
    entries = scale * jax.random.normal(key, dims, jnp.float32)
    if shards:
        entries = entries * block_scale(key, dims, shards, -0.22, 0.18)
    return jnp.clip(entries, -reach, reach).astype(kind)


def setup_inputs(seed: int = 0, part: int = 0) -> dict:
    key_list = jax.random.split(jax.random.key(seed), 10)
    part_keys = jax.random.split(jax.random.fold_in(key_list[9], part), 10)
    return {
        "frames": gaussian(part_keys[0], (TFRAMES, CIN, POS), 1.0, 6.0, ((0, 16),)),
        "clip_lengths": draw_clip_lengths(jax.random.fold_in(jax.random.fold_in(key_list[9], part), 71), part),
        "sequence_slot_map": draw_sequence_slot_map(jax.random.fold_in(jax.random.fold_in(key_list[9], part), 71), part),
        "stem_weight": gaussian(key_list[3], (C1, CIN), CIN ** -0.5, 0.875),
        "time_weight": gaussian(key_list[4], (3, C1, C1), (3 * C1) ** -0.5, 0.3125),
        "norm_gain": jnp.clip(1.0 + 0.18 * jax.random.normal(key_list[5], (C1,), jnp.float32), 0.1, 1.9),
        "mid_weight": gaussian(key_list[6], (C2, C1 * 16), (C1 * 16) ** -0.5, 0.125),
        "latent_weight": gaussian(key_list[7], (LATC, FRAMES * C2), (FRAMES * C2) ** -0.5, 0.09375),
        "patch_embed_weight": gaussian(key_list[8], (PATCH_FEATURES, DIFFUSION_WIDTH), PATCH_FEATURES ** -0.5, 0.75),
    }


def project(weight, data):
    return jnp.einsum('oc,fcp->fop', weight.astype(jnp.float32), data.astype(jnp.float32))

def encode(slab_frames, prior_frames, valid, keep, stem_weight, time_weight, norm_gain, mid_weight, latent_weight):
    first_section = (project(stem_weight, slab_frames) * valid[:, None, None]).astype(jnp.bfloat16)
    prior = (project(stem_weight, prior_frames) * keep).astype(jnp.bfloat16)
    joined = jnp.concatenate([prior, first_section], axis=0)
    mixed = project(time_weight[0], joined[2:10])
    mixed = mixed + project(time_weight[1], joined[1:9])
    mixed = mixed + project(time_weight[2], joined[0:8])
    meansq = lax.optimization_barrier(jnp.mean(mixed * mixed, axis=1, keepdims=True))
    normed = mixed * lax.rsqrt(meansq + 1e-06) * norm_gain.astype(jnp.float32)[None, :, None]
    activated = (normed * jax.nn.sigmoid(normed)).astype(jnp.bfloat16)
    regrouped = activated.reshape(FRAMES, C1 * 16, LS * LS)
    deep = project(mid_weight, regrouped)
    deep = (deep * jax.nn.sigmoid(deep)).astype(jnp.bfloat16)
    taps = latent_weight.astype(jnp.float32).reshape(LATC, FRAMES, C2)
    latent = jnp.einsum('ofc,fcp->op', taps, deep.astype(jnp.float32)).astype(jnp.bfloat16)
    half = LS // 2
    return latent.reshape(LATC, half, 2, half, 2).transpose(1, 3, 0, 2, 4).reshape(half * half, LATC * 4)

def reference(frames, clip_lengths, sequence_slot_map, stem_weight, time_weight, norm_gain, mid_weight, latent_weight, patch_embed_weight):
    counts = (clip_lengths + 7) // 8
    ends = jnp.cumsum(counts)
    starts = ends - counts
    clip_ids = jnp.arange(CLIPS, dtype=jnp.int32)

    def one_slab(slab):
        which = jnp.sum((ends <= slab).astype(jnp.int32))
        hot = clip_ids == which
        start = jnp.sum(jnp.where(hot, starts, 0))
        length = jnp.sum(jnp.where(hot, clip_lengths, 0))
        live = jnp.clip(length - FRAMES * (slab - start), 0, FRAMES)
        valid = (jnp.arange(FRAMES, dtype=jnp.int32) < live).astype(jnp.float32)
        keep = jnp.where(slab == start, jnp.float32(0.0), jnp.float32(1.0))
        here = lax.dynamic_slice_in_dim(frames, (slab * FRAMES).astype(jnp.int32), FRAMES, 0)
        before = lax.dynamic_slice_in_dim(frames, jnp.maximum(slab * FRAMES - 2, 0).astype(jnp.int32), 2, 0)
        return encode(here, before, valid, keep, stem_weight, time_weight, norm_gain, mid_weight, latent_weight)
    rows = lax.map(one_slab, jnp.arange(N_TOK, dtype=jnp.int32)).reshape(N_TOK * SLAB_ROW_COUNT, LATC * 4)
    embedded_tokens = jnp.dot(rows, patch_embed_weight, preferred_element_type=jnp.float32).astype(jnp.bfloat16)
    return jnp.zeros((N_TOK * SLAB_ROW_COUNT, DIFFUSION_WIDTH), jnp.bfloat16).at[sequence_slot_map].set(embedded_tokens)
```

```python
import functools

import jax
import jax.numpy as jnp
from jax import lax
from jax.experimental import pallas as pl
from jax.experimental.pallas import tpu as pltpu
from jax.sharding import PartitionSpec as P

LS = 16
F32 = jnp.float32
BF16 = jnp.bfloat16


def iota(shape, dimension):
    return lax.broadcasted_iota(jnp.int32, shape, dimension)


def dot(a, b):
    return jnp.dot(a, b, preferred_element_type=F32)


def band_weights(stem, time, wband, tiles):
    channels, cin = stem.shape
    taps = time.shape[0]
    window = taps + 1
    rows = iota((cin, window * cin), 0)
    columns = iota((cin, window * cin), 1)
    spread = [
        dot(stem, (columns == rows + j * cin).astype(BF16)).astype(BF16) for j in range(window)
    ]
    for half in range(2):
        total = None
        for k in range(taps):
            part = dot(time[k], spread[taps - 1 - k + half])
            total = part if total is None else total + part
        wband[half * channels : (half + 1) * channels, :] = total


def clip_state(clip_ref, slab, count_frames, clips):
    live = jnp.int32(0)
    first = jnp.int32(0)
    end = jnp.int32(0)
    for c in range(clips):
        length = clip_ref[c]
        begin = end
        end = begin + (length + (count_frames - 1)) // count_frames
        mine = jnp.logical_and(slab >= begin, slab < end)
        left = jnp.clip(length - count_frames * (slab - begin), 0, count_frames)
        live = jnp.where(mine, left, live)
        first = jnp.where(mine, (slab == begin).astype(jnp.int32), first)
    return live, first


def routed(latent, slots_ref, ndev, capacity, side):
    channels, cells = latent.shape
    rows = slots_ref.shape[1]
    half = side // 2
    slots = slots_ref[...].astype(F32)
    target_row = jnp.floor(slots / rows)
    i0, i1 = iota((rows, rows), 0), iota((rows, rows), 1)
    slot_col = jnp.sum(jnp.where(i0 == i1, jnp.broadcast_to(slots, (rows, rows)), 0.0), axis=1, keepdims=True)
    target_col = jnp.floor(slot_col / rows)
    place_col = slot_col - target_col * rows
    same = jnp.logical_and(target_col == target_row, i1 < i0)
    rank = jnp.sum(jnp.where(same, 1.0, 0.0), axis=1, keepdims=True)
    send_col = target_col * capacity + rank
    cell = iota((rows, cells), 1)
    row_of_cell = (cell // (2 * side)) * half + (cell % side) // 2
    mine = row_of_cell == iota((rows, cells), 0)
    send = jnp.sum(jnp.where(mine, send_col, 0.0), axis=0, keepdims=True)
    place = jnp.sum(jnp.where(mine, place_col, 0.0), axis=0, keepdims=True)
    lanes = 128
    pick = (iota((ndev * capacity, cells), 0).astype(F32) == send).astype(BF16)
    feature, cell = iota((lanes, cells), 0), iota((lanes, cells), 1)
    sub = (cell // side) % 2 * 2 + cell % 2
    spread = (iota((lanes, channels), 0) // 4 == iota((lanes, channels), 1)).astype(BF16)
    values = dot(spread, latent)
    values = jnp.where(feature % 4 == sub, values, 0.0)
    tags = jnp.where(jnp.logical_and(feature == 4 * channels, sub == 0), place + 1.0, 0.0)
    values = (values + tags).astype(BF16)
    return lax.dot_general(pick, values, (((1,), (1,)), ((), ())), preferred_element_type=F32).astype(BF16)


def encode_kernel(
    ndev,
    capacity,
    side,
    clips,
    slab_ref,
    clip_ref,
    prior_ref,
    frames_ref,
    slots_ref,
    stem_ref,
    time_ref,
    gain_ref,
    mid_ref,
    latent_ref,
    out_ref,
    joined,
    wband,
    wmask,
    midp,
    regrouped,
    total,
):
    count_frames, cin, positions = frames_ref.shape
    taps = time_ref.shape[0]
    channels = stem_ref.shape[0]
    deep = mid_ref.shape[0]
    cells = side * side
    patches = positions // cells
    pairs = count_frames // 2
    block = 16
    live, first = clip_state(clip_ref, slab_ref[0], count_frames, clips)
    band_weights(stem_ref[...], time_ref[...], wband, None)
    frame_of = iota((2 * channels, 4 * cin), 1)
    offset = (
        (frame_of >= cin).astype(jnp.int32)
        + (frame_of >= 2 * cin).astype(jnp.int32)
        + (frame_of >= 3 * cin).astype(jnp.int32)
        - 2
    )
    for p in range(pairs):
        at = offset + 2 * p
        kept = jnp.where(at < 0, 1 - first, (at < live).astype(jnp.int32))
        wmask[p] = jnp.where(kept > 0, wband[...], 0.0).astype(BF16)
    joined[0 : 2 * cin, :] = prior_ref[...].reshape(2 * cin, positions)
    for f in range(count_frames):
        joined[(2 + f) * cin : (3 + f) * cin, :] = frames_ref[f]
    width = block * patches
    i0, i1 = iota((width, width), 0), iota((width, width), 1)
    permute = (i0 == (i1 % block) * patches + i1 // block).astype(BF16)
    for b in range(channels // block):
        midp[:, b * width : (b + 1) * width] = dot(mid_ref[:, b * width : (b + 1) * width], permute).astype(BF16)
    gain = gain_ref[...] * 0.5
    total[...] = jnp.zeros_like(total)

    def pair(p, carry):
        start = pl.multiple_of(p * 2 * cin, 2 * cin)
        for ab in range(patches):
            mixed = dot(wmask[p], joined[pl.ds(start, 4 * cin), ab * cells : (ab + 1) * cells])
            for half in range(2):
                h = mixed[half * channels : (half + 1) * channels]
                meansq = jnp.sum(h * h, axis=0, keepdims=True) * (1.0 / channels)
                v = h * lax.rsqrt(meansq + 1e-06) * gain
                u = (v * jnp.tanh(v) + v).astype(BF16)
                for b in range(channels // block):
                    row = (b * patches + ab) * block
                    regrouped[row : row + block, half * cells : (half + 1) * cells] = u[
                        b * block : (b + 1) * block
                    ]
        g = dot(midp[...], regrouped[...]) * 0.5
        m = (g * jnp.tanh(g) + g).astype(BF16)
        for half in range(2):
            at = pl.multiple_of((2 * p + half) * deep, deep)
            total[...] += dot(latent_ref[:, pl.ds(at, deep)], m[:, half * cells : (half + 1) * cells])
        return carry

    lax.fori_loop(0, pairs, pair, 0)
    out_ref[...] = routed(total[...].astype(BF16), slots_ref, ndev, capacity, side)


def embed_kernel(incoming_ref, weight_ref, out_ref):
    rows = out_ref.shape[0]
    features = weight_ref.shape[0]
    incoming = incoming_ref[...]
    tags = incoming[:, features : features + 1].astype(F32)
    arrange = (tags == (iota((incoming.shape[0], rows), 1) + 1).astype(F32)).astype(BF16)
    placed = lax.dot_general(arrange, incoming, (((0,), (0,)), ((), ())), preferred_element_type=F32)
    out_ref[...] = dot(placed[:, :features].astype(BF16), weight_ref[...]).astype(BF16)


def per_device(
    frames,
    clip_lengths,
    sequence_slot_map,
    stem_weight,
    time_weight,
    norm_gain,
    mid_weight,
    latent_weight,
    patch_embed_weight,
):
    slab = lax.axis_index("tok")
    ndev = lax.axis_size("tok")
    count_frames, cin, positions = frames.shape
    rows_count = sequence_slot_map.shape[0]
    capacity = max(2, 2 * rows_count // ndev)
    side = LS
    channels = stem_weight.shape[0]
    latents = latent_weight.shape[0]
    deep = mid_weight.shape[0]
    prior = lax.ppermute(frames[count_frames - 2 :], "tok", [(i, i + 1) for i in range(ndev - 1)])
    vmem = pl.BlockSpec(memory_space=pltpu.VMEM)
    smem = pl.BlockSpec(memory_space=pltpu.SMEM)
    outgoing = pl.pallas_call(
        functools.partial(encode_kernel, ndev, capacity, side, clip_lengths.shape[0]),
        out_shape=jax.ShapeDtypeStruct((ndev * capacity, 128), BF16),
        in_specs=[smem, smem] + [vmem] * 8,
        out_specs=vmem,
        scratch_shapes=[
            pltpu.VMEM(((count_frames + 2) * cin, positions), BF16),
            pltpu.VMEM((2 * channels, 4 * cin), F32),
            pltpu.VMEM((count_frames // 2, 2 * channels, 4 * cin), BF16),
            pltpu.VMEM(mid_weight.shape, BF16),
            pltpu.VMEM((mid_weight.shape[1], 2 * side * side), BF16),
            pltpu.VMEM((latents, side * side), F32),
        ],
        compiler_params=pltpu.CompilerParams(vmem_limit_bytes=56 << 20),
        name="encode",
    )(
        slab.astype(jnp.int32).reshape(1),
        clip_lengths,
        prior,
        frames,
        sequence_slot_map.reshape(1, rows_count),
        stem_weight,
        time_weight,
        norm_gain.reshape(channels, 1),
        mid_weight,
        latent_weight,
    )
    incoming = lax.all_to_all(
        outgoing.reshape(ndev, capacity, 128), "tok", split_axis=0, concat_axis=0, tiled=True
    )
    return pl.pallas_call(
        embed_kernel,
        out_shape=jax.ShapeDtypeStruct((rows_count, patch_embed_weight.shape[1]), BF16),
        in_specs=[vmem, vmem],
        out_specs=vmem,
        name="embed",
    )(incoming.reshape(ndev * capacity, 128), patch_embed_weight)


def solution(mesh):
    placed = (
        P(("grp", "tok"), None, None),
        P("grp"),
        P(("grp", "tok")),
        P(),
        P(),
        P(),
        P(),
        P(),
        P(),
    )
    return jax.shard_map(
        per_device, mesh=mesh, in_specs=placed, out_specs=P(("grp", "tok"), None), check_vma=False
    )
```

```python
import functools

import jax
import jax.numpy as jnp
from jax import lax
from jax.experimental import pallas as pl
from jax.experimental.pallas import tpu as pltpu
from jax.sharding import PartitionSpec as P

LS = 16
VMEM_BYTES = 24 << 20
F32 = jnp.float32
BF16 = jnp.bfloat16


def iota(shape, dimension):
    return lax.broadcasted_iota(jnp.int32, shape, dimension)


def dot(a, b):
    return jnp.dot(a, b, preferred_element_type=F32)


def band_weights(stem_ref, time_ref):
    cin, channels = stem_ref.shape
    taps = time_ref.shape[0]
    window = taps + 1
    rows = iota((cin, window * cin), 0)
    columns = iota((cin, window * cin), 1)
    spread = []
    for j in range(window):
        place = (columns == rows + j * cin).astype(BF16)
        spread.append(
            lax.dot_general(
                stem_ref[...], place, (((0,), (0,)), ((), ())), preferred_element_type=F32
            ).astype(BF16)
        )
    halves = []
    for half in range(2):
        total = None
        for k in range(taps):
            part = dot(time_ref[k], spread[taps - 1 - k + half])
            total = part if total is None else total + part
        halves.append(total)
    return jnp.concatenate(halves, axis=0)


def masked(band, first, live, pair, cin):
    column = iota(band.shape, 1)
    at = (
        (column >= cin).astype(jnp.int32)
        + (column >= 2 * cin).astype(jnp.int32)
        + (column >= 3 * cin).astype(jnp.int32)
        + (2 * pair - 2)
    )
    kept = jnp.where(at < 0, 1 - first, (at < live).astype(jnp.int32))
    return jnp.where(kept > 0, band, 0.0).astype(BF16)


def permuted(mid_ref, midp, patches, block):
    width = block * patches
    i0, i1 = iota((width, width), 0), iota((width, width), 1)
    permute = (i0 == (i1 % block) * patches + i1 // block).astype(BF16)
    for b in range(mid_ref.shape[1] // width):
        at = slice(b * width, (b + 1) * width)
        midp[:, at] = dot(mid_ref[:, at], permute).astype(BF16)


def column_of(row):
    n = row.shape[1]
    return jnp.sum(
        jnp.where(iota((n, n), 0) == iota((n, n), 1), jnp.broadcast_to(row, (n, n)), 0.0),
        axis=1,
        keepdims=True,
    )


def activate(mixed, gain, regrouped, ab, patches, block):
    channels = gain.shape[0]
    cells = mixed.shape[1]
    for half in range(2):
        h = mixed[half * channels : (half + 1) * channels]
        meansq = jnp.sum(h * h, axis=0, keepdims=True) * (1.0 / channels)
        v = h * lax.rsqrt(meansq + 1e-06) * gain
        u = (v * jnp.tanh(v) + v).astype(BF16)
        for b in range(channels // block):
            row = (b * patches + ab) * block
            regrouped[row : row + block, half * cells : (half + 1) * cells] = u[
                b * block : (b + 1) * block
            ]


def deepen(midp, regrouped, taps):
    g = dot(midp[...], regrouped[...]) * 0.5
    m = (g * jnp.tanh(g) + g).astype(BF16)
    deep, cells = m.shape[0], m.shape[1] // 2
    return dot(taps[0], m[:, :cells]) + dot(taps[1], m[:, cells:])


def clip_state(clip_ref, slab, count_frames, clips):
    live = jnp.int32(0)
    first = jnp.int32(0)
    end = jnp.int32(0)
    for c in range(clips):
        length = clip_ref[c]
        begin = end
        end = begin + (length + (count_frames - 1)) // count_frames
        mine = jnp.logical_and(slab >= begin, slab < end)
        left = jnp.clip(length - count_frames * (slab - begin), 0, count_frames)
        live = jnp.where(mine, left, live)
        first = jnp.where(mine, (slab == begin).astype(jnp.int32), first)
    return live, first


def routed(latent, slots_ref, ndev, capacity, side):
    channels, cells = latent.shape
    rows = slots_ref.shape[1]
    half = side // 2
    slots = slots_ref[...].astype(F32)
    target_row = jnp.floor(slots / rows)
    i0, i1 = iota((rows, rows), 0), iota((rows, rows), 1)
    slot_col = jnp.sum(jnp.where(i0 == i1, jnp.broadcast_to(slots, (rows, rows)), 0.0), axis=1, keepdims=True)
    target_col = jnp.floor(slot_col / rows)
    place_col = slot_col - target_col * rows
    same = jnp.logical_and(target_col == target_row, i1 < i0)
    rank = jnp.sum(jnp.where(same, 1.0, 0.0), axis=1, keepdims=True)
    send_col = target_col * capacity + rank
    cell = iota((rows, cells), 1)
    row_of_cell = (cell // (2 * side)) * half + (cell % side) // 2
    mine = row_of_cell == iota((rows, cells), 0)
    send = jnp.sum(jnp.where(mine, send_col, 0.0), axis=0, keepdims=True)
    place = jnp.sum(jnp.where(mine, place_col, 0.0), axis=0, keepdims=True)
    lanes = 128
    pick = (iota((ndev * capacity, cells), 0).astype(F32) == send).astype(BF16)
    feature, cell = iota((lanes, cells), 0), iota((lanes, cells), 1)
    sub = (cell // side) % 2 * 2 + cell % 2
    spread = (iota((lanes, channels), 0) // 4 == iota((lanes, channels), 1)).astype(BF16)
    values = dot(spread, latent)
    values = jnp.where(feature % 4 == sub, values, 0.0)
    tags = jnp.where(jnp.logical_and(feature == 4 * channels, sub == 0), place + 1.0, 0.0)
    values = (values + tags).astype(BF16)
    return lax.dot_general(pick, values, (((1,), (1,)), ((), ())), preferred_element_type=F32).astype(BF16)


def rest_kernel(
    clips, slab_ref, clip_ref, frames_ref, stem_ref, time_ref, gain_ref, mid_ref, latent_ref,
    total_ref, midp, wfirst_ref, wmask, regrouped,
):
    cin = stem_ref.shape[0]
    count_frames = frames_ref.shape[0] // cin
    deep = mid_ref.shape[0]
    channels = stem_ref.shape[1]
    patches = mid_ref.shape[1] // channels
    cells = frames_ref.shape[1] // patches
    pairs = count_frames // 2
    block = 16
    live, first = clip_state(clip_ref, slab_ref[0], count_frames, clips)
    band = band_weights(stem_ref, time_ref)
    wfirst_ref[...] = masked(band, first, live, 0, cin)
    for p in range(1, pairs):
        wmask[p - 1] = masked(band, first, live, p, cin)
    permuted(mid_ref, midp, patches, block)
    gain = column_of(gain_ref[...]) * 0.5
    total_ref[...] = jnp.zeros_like(total_ref)

    def pair(p, carry):
        start = pl.multiple_of((p - 1) * 2 * cin, 2 * cin)
        for ab in range(patches):
            mixed = dot(wmask[p - 1], frames_ref[pl.ds(start, 4 * cin), ab * cells : (ab + 1) * cells])
            activate(mixed, gain, regrouped, ab, patches, block)
        taps = [
            latent_ref[:, pl.ds(pl.multiple_of((2 * p + half) * deep, deep), deep)]
            for half in range(2)
        ]
        total_ref[...] += deepen(midp, regrouped, taps)
        return carry

    lax.fori_loop(1, pairs, pair, 0)


def first_kernel(
    ndev, capacity, side, prior_ref, frames_ref, slots_ref, gain_ref, latent_ref, total_ref, midp,
    wfirst_ref, out_ref, regrouped,
):
    channels = gain_ref.shape[1]
    deep = midp.shape[0]
    patches = midp.shape[1] // channels
    cells = prior_ref.shape[1] // patches
    half_rows = prior_ref.shape[0]
    gain = column_of(gain_ref[...]) * 0.5
    for ab in range(patches):
        at = slice(ab * cells, (ab + 1) * cells)
        mixed = dot(wfirst_ref[:, :half_rows], prior_ref[:, at]) + dot(
            wfirst_ref[:, half_rows:], frames_ref[0:half_rows, at]
        )
        activate(mixed, gain, regrouped, ab, patches, 16)
    latent = total_ref[...] + deepen(
        midp, regrouped, [latent_ref[:, :deep], latent_ref[:, deep : 2 * deep]]
    )
    out_ref[...] = routed(latent.astype(BF16), slots_ref, ndev, capacity, side)


def embed_kernel(incoming_ref, weight_ref, out_ref):
    rows = out_ref.shape[0]
    features = weight_ref.shape[0]
    incoming = incoming_ref[...]
    tags = incoming[:, features : features + 1].astype(F32)
    arrange = (tags == (iota((incoming.shape[0], rows), 1) + 1).astype(F32)).astype(BF16)
    placed = lax.dot_general(arrange, incoming, (((0,), (0,)), ((), ())), preferred_element_type=F32)
    out_ref[...] = dot(placed[:, :features].astype(BF16), weight_ref[...]).astype(BF16)


def per_device(
    frames,
    clip_lengths,
    sequence_slot_map,
    stem_weight,
    time_weight,
    norm_gain,
    mid_weight,
    latent_weight,
    patch_embed_weight,
):
    slab = lax.axis_index("tok")
    ndev = lax.axis_size("tok")
    count_frames, cin, positions = frames.shape
    rows_count = sequence_slot_map.shape[0]
    capacity = max(2, 2 * rows_count // ndev)
    side = LS
    channels = stem_weight.shape[0]
    latents = latent_weight.shape[0]
    deep = mid_weight.shape[0]
    prior = lax.ppermute(frames[count_frames - 2 :], "tok", [(i, i + 1) for i in range(ndev - 1)])
    vmem = pl.BlockSpec(memory_space=pltpu.VMEM)
    smem = pl.BlockSpec(memory_space=pltpu.SMEM)
    stacked = frames.reshape(count_frames * cin, positions)
    gain = norm_gain.reshape(1, channels)
    cells = side * side
    flops = 2 * positions * 2 * channels * 4 * cin + 4 * deep * cells * mid_weight.shape[1]
    regrouped = pltpu.VMEM((mid_weight.shape[1], 2 * cells), BF16)
    total, midp, wfirst = pl.pallas_call(
        functools.partial(rest_kernel, clip_lengths.shape[0]),
        out_shape=[
            jax.ShapeDtypeStruct((latents, cells), F32),
            jax.ShapeDtypeStruct(mid_weight.shape, BF16),
            jax.ShapeDtypeStruct((2 * channels, 4 * cin), BF16),
        ],
        in_specs=[smem, smem] + [vmem] * 6,
        out_specs=[vmem] * 3,
        scratch_shapes=[
            pltpu.VMEM((count_frames // 2 - 1, 2 * channels, 4 * cin), BF16),
            regrouped,
        ],
        compiler_params=pltpu.CompilerParams(vmem_limit_bytes=VMEM_BYTES),
        cost_estimate=pl.CostEstimate(
            flops=3 * flops, bytes_accessed=10 << 20, transcendentals=3 * positions * 256
        ),
        name="rest",
    )(
        slab.astype(jnp.int32).reshape(1),
        clip_lengths,
        stacked,
        stem_weight.T,
        time_weight,
        gain,
        mid_weight,
        latent_weight,
    )
    outgoing = pl.pallas_call(
        functools.partial(first_kernel, ndev, capacity, side),
        out_shape=jax.ShapeDtypeStruct((ndev * capacity, 128), BF16),
        in_specs=[vmem] * 8,
        out_specs=vmem,
        scratch_shapes=[regrouped],
        compiler_params=pltpu.CompilerParams(vmem_limit_bytes=VMEM_BYTES),
        name="first",
    )(
        prior.reshape(2 * cin, positions),
        stacked,
        sequence_slot_map.reshape(1, rows_count),
        gain,
        latent_weight,
        total,
        midp,
        wfirst,
    )
    incoming = lax.all_to_all(
        outgoing.reshape(ndev, capacity, 128), "tok", split_axis=0, concat_axis=0, tiled=True
    )
    return pl.pallas_call(
        embed_kernel,
        out_shape=jax.ShapeDtypeStruct((rows_count, patch_embed_weight.shape[1]), BF16),
        in_specs=[vmem, vmem],
        out_specs=vmem,
        name="embed",
    )(incoming.reshape(ndev * capacity, 128), patch_embed_weight)


def solution(mesh):
    placed = (
        P(("grp", "tok"), None, None),
        P("grp"),
        P(("grp", "tok")),
        P(),
        P(),
        P(),
        P(),
        P(),
        P(),
    )
    return jax.shard_map(
        per_device, mesh=mesh, in_specs=placed, out_specs=P(("grp", "tok"), None), check_vma=False
    )
```

```python
import functools

import jax
import jax.numpy as jnp
from jax import lax
from jax.experimental import pallas as pl
from jax.experimental.pallas import tpu as pltpu
from jax.sharding import PartitionSpec as P

LS = 16
VMEM_BYTES = 24 << 20
F32 = jnp.float32
BF16 = jnp.bfloat16


def iota(shape, dimension):
    return lax.broadcasted_iota(jnp.int32, shape, dimension)


def dot(a, b):
    return jnp.dot(a, b, preferred_element_type=F32)


def band_weights(stem_ref, time_ref):
    cin, channels = stem_ref.shape
    taps = time_ref.shape[0]
    window = taps + 1
    rows = iota((cin, window * cin), 0)
    columns = iota((cin, window * cin), 1)
    spread = []
    for j in range(window):
        place = (columns == rows + j * cin).astype(BF16)
        spread.append(
            lax.dot_general(
                stem_ref[...], place, (((0,), (0,)), ((), ())), preferred_element_type=F32
            ).astype(BF16)
        )
    halves = []
    for half in range(2):
        total = None
        for k in range(taps):
            part = dot(time_ref[k], spread[taps - 1 - k + half])
            total = part if total is None else total + part
        halves.append(total)
    return jnp.concatenate(halves, axis=0)


def masked(band, first, live, pair, cin):
    column = iota(band.shape, 1)
    at = (
        (column >= cin).astype(jnp.int32)
        + (column >= 2 * cin).astype(jnp.int32)
        + (column >= 3 * cin).astype(jnp.int32)
        + (2 * pair - 2)
    )
    kept = jnp.where(at < 0, 1 - first, (at < live).astype(jnp.int32))
    return jnp.where(kept > 0, band, 0.0).astype(BF16)


def permuted(mid_ref, midp, patches, block):
    width = block * patches
    i0, i1 = iota((width, width), 0), iota((width, width), 1)
    permute = jnp.where(i0 == (i1 % block) * patches + i1 // block, 0.5, 0.0).astype(BF16)
    for b in range(mid_ref.shape[1] // width):
        at = slice(b * width, (b + 1) * width)
        midp[:, at] = dot(mid_ref[:, at], permute).astype(BF16)


def column_of(row):
    n = row.shape[1]
    return jnp.sum(
        jnp.where(iota((n, n), 0) == iota((n, n), 1), jnp.broadcast_to(row, (n, n)), 0.0),
        axis=1,
        keepdims=True,
    )


def activate(weights, window, gain, half, regrouped, shape):
    channels, patches, block = shape
    lanes = window(0, half).shape[1]
    for j in range(0, patches, 2):
        data = jnp.concatenate([window(j, half), window(j + 1, half)], axis=1)
        mixed = dot(weights, data)
        sides = []
        for f in range(2):
            h = mixed[f * channels : (f + 1) * channels]
            meansq = jnp.sum(h * h, axis=0, keepdims=True) * (1.0 / channels)
            v = h * lax.rsqrt(meansq + 1e-06) * gain
            sides.append((v * jnp.tanh(v) + v).astype(BF16))
        for a in range(2):
            at = slice(a * lanes, (a + 1) * lanes)
            u = jnp.concatenate([side[:, at] for side in sides], axis=1)
            for b in range(channels // block):
                row = (b * patches + j + a) * block
                regrouped[row : row + block, :] = u[b * block : (b + 1) * block, :]


def deepen(midp, regrouped, taps):
    rows = midp.shape[0] // 2
    parts = []
    for at in range(2):
        g = dot(midp[at * rows : (at + 1) * rows], regrouped[...])
        parts.append((g * jnp.tanh(g) + g).astype(BF16))
    both = dot(taps, jnp.concatenate(parts, axis=0))
    rows, lanes = both.shape[0] // 2, both.shape[1] // 2
    return both[:rows, :lanes] + both[rows:, lanes:]


def clip_state(clip_ref, slab, count_frames, clips):
    live = jnp.int32(0)
    first = jnp.int32(0)
    end = jnp.int32(0)
    for c in range(clips):
        length = clip_ref[c]
        begin = end
        end = begin + (length + (count_frames - 1)) // count_frames
        mine = jnp.logical_and(slab >= begin, slab < end)
        left = jnp.clip(length - count_frames * (slab - begin), 0, count_frames)
        live = jnp.where(mine, left, live)
        first = jnp.where(mine, (slab == begin).astype(jnp.int32), first)
    return live, first


def routing(slots_ref, ndev, capacity, side, channels):
    rows = slots_ref.shape[1]
    cells = side * side
    half = side // 2
    slots = slots_ref[...].astype(F32)
    target_row = jnp.floor(slots / rows)
    i0, i1 = iota((rows, rows), 0), iota((rows, rows), 1)
    slot_col = column_of(slots)
    target_col = jnp.floor(slot_col / rows)
    place_col = slot_col - target_col * rows
    same = jnp.logical_and(target_col == target_row, i1 < i0)
    rank = jnp.sum(jnp.where(same, 1.0, 0.0), axis=1, keepdims=True)
    send_col = target_col * capacity + rank
    cell = iota((rows, cells), 1)
    row_of_cell = (cell // (2 * side)) * half + (cell % side) // 2
    mine = row_of_cell == iota((rows, cells), 0)
    send = jnp.sum(jnp.where(mine, send_col, 0.0), axis=0, keepdims=True)
    place = jnp.sum(jnp.where(mine, place_col, 0.0), axis=0, keepdims=True)
    pick = (iota((ndev * capacity, cells), 0).astype(F32) == send).astype(BF16)
    feature, cell = iota((128, cells), 0), iota((128, cells), 1)
    sub = (cell // side) % 2 * 2 + cell % 2
    tags = jnp.where(jnp.logical_and(feature == 4 * channels, sub == 0), place + 1.0, 0.0)
    return pick, tags


def routed(latent, pick, tags, side):
    channels, cells = latent.shape
    feature, cell = iota((128, cells), 0), iota((128, cells), 1)
    sub = (cell // side) % 2 * 2 + cell % 2
    spread = (iota((128, channels), 0) // 4 == iota((128, channels), 1)).astype(BF16)
    values = (jnp.where(feature % 4 == sub, dot(spread, latent), 0.0) + tags).astype(BF16)
    return lax.dot_general(pick, values, (((1,), (1,)), ((), ())), preferred_element_type=F32).astype(BF16)


def frame_taps(latent_ref, pair, deep):
    at = 2 * pair * deep
    return jnp.concatenate(
        [latent_ref[:, at : at + deep], latent_ref[:, at + deep : at + 2 * deep]], axis=0
    )


def rest_kernel(
    ndev, capacity, side, clips, slab_ref, clip_ref, slots_hbm, frames_hbm, stem_hbm, time_hbm, gain_hbm, mid_hbm, latent_hbm,
    total_ref, midp, wfirst_ref, pick_ref, tags_ref, slots_ref, stem_ref, time_ref, gain_ref, frames_ref, mid_ref, latent_ref,
    even, odd, sems,
):
    cin, channels = stem_ref.shape
    count_frames = frames_ref.shape[0] // cin
    deep = mid_ref.shape[0]
    patches = mid_ref.shape[1] // channels
    cells = frames_ref.shape[1] // patches
    lanes = cells // 2
    block = 16
    window = 4 * cin
    moves = [
        (slots_hbm, slots_ref),
        (stem_hbm, stem_ref),
        (time_hbm, time_ref),
        (gain_hbm, gain_ref),
        (frames_hbm.at[0:window], frames_ref.at[0:window]),
        (mid_hbm, mid_ref),
        (frames_hbm.at[window:], frames_ref.at[window:]),
        (latent_hbm, latent_ref),
    ]
    copies = [pltpu.make_async_copy(a, b, sems.at[i]) for i, (a, b) in enumerate(moves)]
    for copy in copies:
        copy.start()
    live, first = clip_state(clip_ref, slab_ref[0], count_frames, clips)
    for copy in copies[:4]:
        copy.wait()
    pick_ref[...], tags_ref[...] = routing(slots_ref, ndev, capacity, side, latent_ref.shape[0])
    band = band_weights(stem_ref, time_ref)
    gain = column_of(gain_ref[...]) * 0.5
    wfirst_ref[...] = masked(band, first, live, 0, cin)
    for copy in copies[4:]:
        copy.wait()
    permuted(mid_ref, midp, patches, block)
    units = [(p, half) for p in range(1, count_frames // 2) for half in range(2)]
    buffers = [even, odd]
    sums = [None, None]

    def work(q):
        p, half = units[q]
        start = (p - 1) * 2 * cin

        def at(ab, half):
            low = ab * cells + half * lanes
            return frames_ref[start : start + window, low : low + lanes]

        activate(masked(band, first, live, p, cin), at, gain, half, buffers[q % 2], (channels, patches, block))

    def finish(q):
        p, half = units[q]
        part = deepen(midp, buffers[q % 2], frame_taps(latent_ref, p, deep))
        sums[half] = part if sums[half] is None else sums[half] + part

    work(0)
    for q in range(1, len(units)):
        work(q)
        finish(q - 1)
    finish(len(units) - 1)
    total_ref[...] = jnp.concatenate(sums, axis=1)


def first_kernel(
    side, prior_ref, frames_ref, gain_ref, latent_ref, total_ref, midp, wfirst_ref, pick_ref, tags_ref,
    out_ref, even, odd,
):
    channels = gain_ref.shape[1]
    deep = midp.shape[0]
    patches = midp.shape[1] // channels
    cells = prior_ref.shape[1] // patches
    lanes = cells // 2
    rows = prior_ref.shape[0]
    gain = column_of(gain_ref[...]) * 0.5

    def at(ab, half):
        low = ab * cells + half * lanes
        return jnp.concatenate(
            [prior_ref[:, low : low + lanes], frames_ref[0:rows, low : low + lanes]], axis=0
        )

    shape = (channels, patches, 16)
    taps = frame_taps(latent_ref, 0, deep)
    activate(wfirst_ref[...], at, gain, 0, even, shape)
    activate(wfirst_ref[...], at, gain, 1, odd, shape)
    sums = [deepen(midp, even, taps), deepen(midp, odd, taps)]
    latent = total_ref[...] + jnp.concatenate(sums, axis=1)
    out_ref[...] = routed(latent.astype(BF16), pick_ref[...], tags_ref[...], side)


def embed_kernel(incoming_ref, weight_ref, out_ref):
    rows = out_ref.shape[0]
    features = weight_ref.shape[0]
    incoming = incoming_ref[...]
    tags = incoming[:, features : features + 1].astype(F32)
    arrange = (tags == (iota((incoming.shape[0], rows), 1) + 1).astype(F32)).astype(BF16)
    placed = lax.dot_general(arrange, incoming, (((0,), (0,)), ((), ())), preferred_element_type=F32)
    out_ref[...] = dot(placed[:, :features].astype(BF16), weight_ref[...]).astype(BF16)


def per_device(
    frames,
    clip_lengths,
    sequence_slot_map,
    stem_weight,
    time_weight,
    norm_gain,
    mid_weight,
    latent_weight,
    patch_embed_weight,
):
    slab = lax.axis_index("tok")
    ndev = lax.axis_size("tok")
    count_frames, cin, positions = frames.shape
    rows_count = sequence_slot_map.shape[0]
    capacity = max(2, 2 * rows_count // ndev)
    side = LS
    channels = stem_weight.shape[0]
    latents = latent_weight.shape[0]
    deep = mid_weight.shape[0]
    prior = lax.ppermute(frames[count_frames - 2 :], "tok", [(i, i + 1) for i in range(ndev - 1)])
    vmem = pl.BlockSpec(memory_space=pltpu.VMEM)
    smem = pl.BlockSpec(memory_space=pltpu.SMEM)
    stacked = frames.reshape(count_frames * cin, positions)
    gain = norm_gain.reshape(1, channels)
    cells = side * side
    flops = 2 * positions * 2 * channels * 4 * cin + 4 * deep * cells * mid_weight.shape[1]
    regrouped = pltpu.VMEM((mid_weight.shape[1], cells), BF16)
    hbm = pl.BlockSpec(memory_space=pltpu.HBM)
    total, midp, wfirst, pick, tags = pl.pallas_call(
        functools.partial(rest_kernel, ndev, capacity, side, clip_lengths.shape[0]),
        out_shape=[
            jax.ShapeDtypeStruct((latents, cells), F32),
            jax.ShapeDtypeStruct(mid_weight.shape, BF16),
            jax.ShapeDtypeStruct((2 * channels, 4 * cin), BF16),
            jax.ShapeDtypeStruct((ndev * capacity, cells), BF16),
            jax.ShapeDtypeStruct((128, cells), F32),
        ],
        in_specs=[smem, smem] + [hbm] * 7,
        out_specs=[vmem] * 5,
        scratch_shapes=[
            pltpu.VMEM((1, rows_count), jnp.int32),
            pltpu.VMEM((cin, channels), BF16),
            pltpu.VMEM(time_weight.shape, BF16),
            pltpu.VMEM((1, channels), F32),
            pltpu.VMEM(stacked.shape, BF16),
            pltpu.VMEM(mid_weight.shape, BF16),
            pltpu.VMEM(latent_weight.shape, BF16),
            regrouped,
            regrouped,
            pltpu.SemaphoreType.DMA((8,)),
        ],
        compiler_params=pltpu.CompilerParams(vmem_limit_bytes=VMEM_BYTES),
        cost_estimate=pl.CostEstimate(
            flops=3 * flops, bytes_accessed=10 << 20, transcendentals=3 * positions * 256
        ),
        name="rest",
    )(
        slab.astype(jnp.int32).reshape(1),
        pltpu.with_memory_space_constraint(clip_lengths, pltpu.HBM),
        *[
            pltpu.with_memory_space_constraint(x, pltpu.HBM)
            for x in (sequence_slot_map.reshape(1, rows_count), stacked, stem_weight.T, time_weight, gain, mid_weight, latent_weight)
        ],
    )
    outgoing = pl.pallas_call(
        functools.partial(first_kernel, side),
        out_shape=jax.ShapeDtypeStruct((ndev * capacity, 128), BF16),
        in_specs=[vmem] * 9,
        out_specs=vmem,
        scratch_shapes=[regrouped, regrouped],
        compiler_params=pltpu.CompilerParams(vmem_limit_bytes=VMEM_BYTES),
        name="first",
    )(
        prior.reshape(2 * cin, positions),
        stacked,
        gain,
        latent_weight,
        total,
        midp,
        wfirst,
        pick,
        tags,
    )
    incoming = lax.all_to_all(
        outgoing.reshape(ndev, capacity, 128), "tok", split_axis=0, concat_axis=0, tiled=True
    )
    return pl.pallas_call(
        embed_kernel,
        out_shape=jax.ShapeDtypeStruct((rows_count, patch_embed_weight.shape[1]), BF16),
        in_specs=[vmem, vmem],
        out_specs=vmem,
        compiler_params=pltpu.CompilerParams(vmem_limit_bytes=4 << 20),
        name="embed",
    )(incoming.reshape(ndev * capacity, 128), patch_embed_weight)


def solution(mesh):
    placed = (
        P(("grp", "tok"), None, None),
        P("grp"),
        P(("grp", "tok")),
        P(),
        P(),
        P(),
        P(),
        P(),
        P(),
    )
    return jax.shard_map(
        per_device, mesh=mesh, in_specs=placed, out_specs=P(("grp", "tok"), None), check_vma=False
    )
```

```python
import functools

import jax
import jax.numpy as jnp
from jax import lax
from jax.experimental import pallas as pl
from jax.experimental.pallas import tpu as pltpu
from jax.sharding import PartitionSpec as P

LS = 16
VMEM_BYTES = 24 << 20
F32 = jnp.float32
BF16 = jnp.bfloat16


def iota(shape, dimension):
    return lax.broadcasted_iota(jnp.int32, shape, dimension)


def dot(a, b):
    return jnp.dot(a, b, preferred_element_type=F32)


def band_weights(stem_ref, time_ref):
    cin, channels = stem_ref.shape
    taps = time_ref.shape[0]
    window = taps + 1
    rows = iota((cin, window * cin), 0)
    columns = iota((cin, window * cin), 1)
    spread = []
    for j in range(window):
        place = (columns == rows + j * cin).astype(BF16)
        spread.append(
            lax.dot_general(
                stem_ref[...], place, (((0,), (0,)), ((), ())), preferred_element_type=F32
            ).astype(BF16)
        )
    halves = []
    for half in range(2):
        total = None
        for k in range(taps):
            part = dot(time_ref[k], spread[taps - 1 - k + half])
            total = part if total is None else total + part
        halves.append(total)
    return jnp.concatenate(halves, axis=0)


def masked(band, first, live, pair, cin):
    column = iota(band.shape, 1)
    at = (
        (column >= cin).astype(jnp.int32)
        + (column >= 2 * cin).astype(jnp.int32)
        + (column >= 3 * cin).astype(jnp.int32)
        + (2 * pair - 2)
    )
    kept = jnp.where(at < 0, 1 - first, (at < live).astype(jnp.int32))
    return jnp.where(kept > 0, band, 0.0).astype(BF16)


def permuted(mid_ref, midp, patches, block):
    width = block * patches
    i0, i1 = iota((width, width), 0), iota((width, width), 1)
    permute = jnp.where(i0 == (i1 % block) * patches + i1 // block, 0.5, 0.0).astype(BF16)
    for b in range(mid_ref.shape[1] // width):
        at = slice(b * width, (b + 1) * width)
        midp[:, at] = dot(mid_ref[:, at], permute).astype(BF16)


def column_of(row):
    n = row.shape[1]
    return jnp.sum(
        jnp.where(iota((n, n), 0) == iota((n, n), 1), jnp.broadcast_to(row, (n, n)), 0.0),
        axis=1,
        keepdims=True,
    )


def activate(weights, window, gain, half, regrouped, shape):
    channels, patches, block = shape
    lanes = window(0, half).shape[1]
    for j in range(0, patches, 2):
        data = jnp.concatenate([window(j, half), window(j + 1, half)], axis=1)
        mixed = dot(weights, data)
        sides = []
        for f in range(2):
            h = mixed[f * channels : (f + 1) * channels]
            meansq = jnp.sum(h * h, axis=0, keepdims=True) * (1.0 / channels)
            v = h * lax.rsqrt(meansq + 1e-06) * gain
            sides.append((v * jnp.tanh(v) + v).astype(BF16))
        for a in range(2):
            at = slice(a * lanes, (a + 1) * lanes)
            u = jnp.concatenate([side[:, at] for side in sides], axis=1)
            for b in range(channels // block):
                row = (b * patches + j + a) * block
                regrouped[row : row + block, :] = u[b * block : (b + 1) * block, :]


def deepen(midp, regrouped, taps):
    rows = midp.shape[0] // 2
    parts = []
    for at in range(2):
        g = dot(midp[at * rows : (at + 1) * rows], regrouped[...])
        parts.append((g * jnp.tanh(g) + g).astype(BF16))
    both = dot(taps, jnp.concatenate(parts, axis=0))
    rows, lanes = both.shape[0] // 2, both.shape[1] // 2
    return both[:rows, :lanes] + both[rows:, lanes:]


def clip_state(clip_ref, slab, count_frames, clips):
    live = jnp.int32(0)
    first = jnp.int32(0)
    end = jnp.int32(0)
    for c in range(clips):
        length = clip_ref[c]
        begin = end
        end = begin + (length + (count_frames - 1)) // count_frames
        mine = jnp.logical_and(slab >= begin, slab < end)
        left = jnp.clip(length - count_frames * (slab - begin), 0, count_frames)
        live = jnp.where(mine, left, live)
        first = jnp.where(mine, (slab == begin).astype(jnp.int32), first)
    return live, first


def routing(slots_ref, ndev, capacity, side, channels):
    rows = slots_ref.shape[1]
    cells = side * side
    half = side // 2
    slots = slots_ref[...].astype(F32)
    target_row = jnp.floor(slots / rows)
    i0, i1 = iota((rows, rows), 0), iota((rows, rows), 1)
    slot_col = column_of(slots)
    target_col = jnp.floor(slot_col / rows)
    place_col = slot_col - target_col * rows
    same = jnp.logical_and(target_col == target_row, i1 < i0)
    rank = jnp.sum(jnp.where(same, 1.0, 0.0), axis=1, keepdims=True)
    send_col = target_col * capacity + rank
    cell = iota((rows, cells), 1)
    row_of_cell = (cell // (2 * side)) * half + (cell % side) // 2
    mine = row_of_cell == iota((rows, cells), 0)
    send = jnp.sum(jnp.where(mine, send_col, 0.0), axis=0, keepdims=True)
    place = jnp.sum(jnp.where(mine, place_col, 0.0), axis=0, keepdims=True)
    pick = (iota((ndev * capacity, cells), 0).astype(F32) == send).astype(BF16)
    feature, cell = iota((128, cells), 0), iota((128, cells), 1)
    sub = (cell // side) % 2 * 2 + cell % 2
    tags = jnp.where(jnp.logical_and(feature == 4 * channels, sub == 0), place + 1.0, 0.0)
    return pick, tags


def routed(latent, pick, tags, side):
    channels, cells = latent.shape
    feature, cell = iota((128, cells), 0), iota((128, cells), 1)
    sub = (cell // side) % 2 * 2 + cell % 2
    spread = (iota((128, channels), 0) // 4 == iota((128, channels), 1)).astype(BF16)
    values = (jnp.where(feature % 4 == sub, dot(spread, latent), 0.0) + tags).astype(BF16)
    return lax.dot_general(pick, values, (((1,), (1,)), ((), ())), preferred_element_type=F32).astype(BF16)


def frame_taps(latent_ref, pair, deep):
    at = 2 * pair * deep
    return jnp.concatenate(
        [latent_ref[:, at : at + deep], latent_ref[:, at + deep : at + 2 * deep]], axis=0
    )


def rest_kernel(
    ndev, capacity, side, clips, slab_ref, clip_hbm, slots_hbm, frames_hbm, stem_hbm, time_hbm, gain_hbm, mid_hbm, latent_hbm,
    total_ref, midp, wfirst_ref, pick_ref, tags_ref, clip_ref, slots_ref, stem_ref, time_ref, gain_ref, frames_ref, mid_ref, latent_ref,
    even, odd, sems,
):
    cin, channels = stem_ref.shape
    count_frames = frames_ref.shape[0] // cin
    deep = mid_ref.shape[0]
    patches = mid_ref.shape[1] // channels
    cells = frames_ref.shape[1] // patches
    lanes = cells // 2
    block = 16
    window = 4 * cin
    moves = [
        (clip_hbm, clip_ref),
        (slots_hbm, slots_ref),
        (stem_hbm, stem_ref),
        (time_hbm, time_ref),
        (gain_hbm, gain_ref),
        (frames_hbm.at[0:window], frames_ref.at[0:window]),
        (mid_hbm, mid_ref),
        (frames_hbm.at[window:], frames_ref.at[window:]),
        (latent_hbm, latent_ref),
    ]
    copies = [pltpu.make_async_copy(a, b, sems.at[i]) for i, (a, b) in enumerate(moves)]
    for copy in copies:
        copy.start()
    for copy in copies[:5]:
        copy.wait()
    live, first = clip_state(clip_ref, slab_ref[0], count_frames, clips)
    pick_ref[...], tags_ref[...] = routing(slots_ref, ndev, capacity, side, latent_ref.shape[0])
    band = band_weights(stem_ref, time_ref)
    gain = column_of(gain_ref[...]) * 0.5
    wfirst_ref[...] = masked(band, first, live, 0, cin)
    copies[5].wait()
    copies[6].wait()
    units = [(p, half) for p in range(1, count_frames // 2) for half in range(2)]
    buffers = [even, odd]
    sums = [None, None]

    def work(q):
        p, half = units[q]
        start = (p - 1) * 2 * cin

        def at(ab, half):
            low = ab * cells + half * lanes
            return frames_ref[start : start + window, low : low + lanes]

        activate(masked(band, first, live, p, cin), at, gain, half, buffers[q % 2], (channels, patches, block))

    def finish(q):
        p, half = units[q]
        part = deepen(midp, buffers[q % 2], frame_taps(latent_ref, p, deep))
        sums[half] = part if sums[half] is None else sums[half] + part

    permuted(mid_ref, midp, patches, block)
    work(0)
    copies[7].wait()
    copies[8].wait()
    for q in range(1, len(units)):
        work(q)
        finish(q - 1)
    finish(len(units) - 1)
    total_ref[...] = jnp.concatenate(sums, axis=1)


def first_kernel(
    side, prior_ref, frames_ref, gain_ref, latent_ref, total_ref, midp, wfirst_ref, pick_ref, tags_ref,
    out_ref, even, odd,
):
    channels = gain_ref.shape[1]
    deep = midp.shape[0]
    patches = midp.shape[1] // channels
    cells = prior_ref.shape[1] // patches
    lanes = cells // 2
    rows = prior_ref.shape[0]
    gain = column_of(gain_ref[...]) * 0.5

    def at(ab, half):
        low = ab * cells + half * lanes
        return jnp.concatenate(
            [prior_ref[:, low : low + lanes], frames_ref[0:rows, low : low + lanes]], axis=0
        )

    shape = (channels, patches, 16)
    taps = frame_taps(latent_ref, 0, deep)
    activate(wfirst_ref[...], at, gain, 0, even, shape)
    activate(wfirst_ref[...], at, gain, 1, odd, shape)
    sums = [deepen(midp, even, taps), deepen(midp, odd, taps)]
    latent = total_ref[...] + jnp.concatenate(sums, axis=1)
    out_ref[...] = routed(latent.astype(BF16), pick_ref[...], tags_ref[...], side)


def embed_kernel(incoming_ref, weight_ref, out_ref):
    rows = out_ref.shape[0]
    features = weight_ref.shape[0]
    incoming = incoming_ref[...]
    tags = incoming[:, features : features + 1].astype(F32)
    arrange = (tags == (iota((incoming.shape[0], rows), 1) + 1).astype(F32)).astype(BF16)
    placed = lax.dot_general(arrange, incoming, (((0,), (0,)), ((), ())), preferred_element_type=F32)
    out_ref[...] = dot(placed[:, :features].astype(BF16), weight_ref[...]).astype(BF16)


def per_device(
    frames,
    clip_lengths,
    sequence_slot_map,
    stem_weight,
    time_weight,
    norm_gain,
    mid_weight,
    latent_weight,
    patch_embed_weight,
):
    slab = lax.axis_index("tok")
    ndev = lax.axis_size("tok")
    count_frames, cin, positions = frames.shape
    rows_count = sequence_slot_map.shape[0]
    capacity = max(2, 2 * rows_count // ndev)
    side = LS
    channels = stem_weight.shape[0]
    latents = latent_weight.shape[0]
    deep = mid_weight.shape[0]
    prior = lax.ppermute(frames[count_frames - 2 :], "tok", [(i, (i + 1) % ndev) for i in range(ndev)])
    vmem = pl.BlockSpec(memory_space=pltpu.VMEM)
    smem = pl.BlockSpec(memory_space=pltpu.SMEM)
    stacked = frames.reshape(count_frames * cin, positions)
    gain = norm_gain.reshape(1, channels)
    cells = side * side
    flops = 2 * positions * 2 * channels * 4 * cin + 4 * deep * cells * mid_weight.shape[1]
    regrouped = pltpu.VMEM((mid_weight.shape[1], cells), BF16)
    hbm = pl.BlockSpec(memory_space=pltpu.HBM)
    total, midp, wfirst, pick, tags = pl.pallas_call(
        functools.partial(rest_kernel, ndev, capacity, side, clip_lengths.shape[0]),
        out_shape=[
            jax.ShapeDtypeStruct((latents, cells), F32),
            jax.ShapeDtypeStruct(mid_weight.shape, BF16),
            jax.ShapeDtypeStruct((2 * channels, 4 * cin), BF16),
            jax.ShapeDtypeStruct((ndev * capacity, cells), BF16),
            jax.ShapeDtypeStruct((128, cells), F32),
        ],
        in_specs=[smem] + [hbm] * 8,
        out_specs=[vmem] * 5,
        scratch_shapes=[
            pltpu.SMEM(clip_lengths.shape, jnp.int32),
            pltpu.VMEM((1, rows_count), jnp.int32),
            pltpu.VMEM((cin, channels), BF16),
            pltpu.VMEM(time_weight.shape, BF16),
            pltpu.VMEM((1, channels), F32),
            pltpu.VMEM(stacked.shape, BF16),
            pltpu.VMEM(mid_weight.shape, BF16),
            pltpu.VMEM(latent_weight.shape, BF16),
            regrouped,
            regrouped,
            pltpu.SemaphoreType.DMA((9,)),
        ],
        compiler_params=pltpu.CompilerParams(
            vmem_limit_bytes=VMEM_BYTES
        ),
        cost_estimate=pl.CostEstimate(
            flops=3 * flops, bytes_accessed=10 << 20, transcendentals=3 * positions * 256
        ),
        name="rest",
    )(
        slab.astype(jnp.int32).reshape(1),
        *[
            pltpu.with_memory_space_constraint(x, pltpu.HBM)
            for x in (
                clip_lengths,
                sequence_slot_map.reshape(1, rows_count),
                stacked,
                stem_weight.T,
                time_weight,
                gain,
                mid_weight,
                latent_weight,
            )
        ],
    )
    outgoing = pl.pallas_call(
        functools.partial(first_kernel, side),
        out_shape=jax.ShapeDtypeStruct((ndev * capacity, 128), BF16),
        in_specs=[vmem] * 9,
        out_specs=vmem,
        scratch_shapes=[regrouped, regrouped],
        compiler_params=pltpu.CompilerParams(
            vmem_limit_bytes=VMEM_BYTES
        ),
        name="first",
    )(
        prior.reshape(2 * cin, positions),
        stacked,
        gain,
        latent_weight,
        total,
        midp,
        wfirst,
        pick,
        tags,
    )
    incoming = lax.all_to_all(
        outgoing.reshape(ndev, capacity, 128), "tok", split_axis=0, concat_axis=0, tiled=True
    )
    return pl.pallas_call(
        embed_kernel,
        out_shape=jax.ShapeDtypeStruct((rows_count, patch_embed_weight.shape[1]), BF16),
        in_specs=[vmem, vmem],
        out_specs=vmem,
        compiler_params=pltpu.CompilerParams(vmem_limit_bytes=4 << 20),
        name="embed",
    )(incoming.reshape(ndev * capacity, 128), patch_embed_weight)


def solution(mesh):
    placed = (
        P(("grp", "tok"), None, None),
        P("grp"),
        P(("grp", "tok")),
        P(),
        P(),
        P(),
        P(),
        P(),
        P(),
    )
    return jax.shard_map(
        per_device, mesh=mesh, in_specs=placed, out_specs=P(("grp", "tok"), None), check_vma=False
    )
```
